32 devices in a mesh: ens: 2 (over y), comp: 4 (over z), lat: 2 (over x), lon: 2 (over core).
Axes of the slice: x: 2, y: 2, z: 4, core: 2. Of those that a mesh axis runs over, the one named last changes fastest.
Arguments:
- spectrum: float32 [2304, 16, 256], P(('ens', 'comp'), 'lat', 'lon'), parts along dimension 0, may hold values from 0 to 2
- sea_mask: int32 [16, 256], P('lat', 'lon'), may hold values 0 or 1
- depth_class: int32 [16, 256], P('lat', 'lon'), may hold values from 0 to 15
- current_class: int32 [16, 256], P('lat', 'lon'), may hold values from 0 to 15
- speed_table: float32 [16, 32], replicated, may hold values from 0.1 to 0.5
- current_table: float32 [16, 2], replicated, may hold values from -0.14 to 0.14
- coupling: float32 [1152], replicated, may hold values from 0.05 to 0.5
- quad_index: int32 [2, 1152, 4], replicated, may hold values from 0 to 1151, as said below
- quad_weight: float32 [2, 1152, 4], replicated, may hold values from 0 to 1, as said below
Outputs:
- spectrum_out: float32 [2304, 16, 256], P(('ens', 'comp'), 'lat', 'lon'), parts along dimension 0
The draws below stay inside these ranges and needn't reach their ends.
There are 2 independent parts, one for each index of `ens`. The reference program is written for one: setup_inputs(seed, part) draws one part's arguments, and reference() takes and returns one part's arrays. A program takes and returns all parts, laid end to end along the dimension named above; an argument that names none is the same for every part. Nothing has to cross between parts.
Inputs may be any that keep to these rules, and one draw needn't show every extreme that they name: `quad_index`: for each side (0 plus, 1 minus) and component k the four entries are distinct components: two adjacent frequencies crossed with two adjacent directions, directions counted modulo 36; a component's number is its frequency times 36 plus its direction. `quad_weight`: the four weights of each side and component are non-negative and sum to one.
All inputs are finite; a program needn't handle non-finite values. No bound on the sum of `sea_mask` on one device may be relied on, other than what follows from the above.
Results may differ from the reference program's by a relative error of at most 0.002.
Values sent between devices are 32-bit elements; how exact they have to be, the bound alone decides.
A program may use at most 64 MiB of HBM per device.

```python
import math
import jax
import jax.numpy as jnp
from jax import lax

NDIR = 36
NFREQ = 32
K = 1152
SUBSTEPS = 4
NDEPTH = 16
NCUR = 16
NLAT = 16
NLON = 256


def quad_corners(key):
    comp_total = NDIR * NFREQ
    comp_ids = jnp.arange(comp_total, dtype=jnp.int32)
    freq_ids = comp_ids // NDIR
    dir_ids = comp_ids % NDIR
    freq_key = jax.random.fold_in(key, 101)
    dir_key = jax.random.fold_in(key, 202)
    freq_step = jax.random.randint(freq_key, (2, NFREQ), 1, 3, dtype=jnp.int32)
    dir_step = jax.random.randint(dir_key, (2, NFREQ), 1, max(2, NDIR // 4), dtype=jnp.int32)
    signs = jnp.array([[1], [-1]], dtype=jnp.int32)
    base_freq = jnp.clip(freq_ids[None] + signs * freq_step[:, freq_ids], 0, NFREQ - 2)
    base_dir = jnp.mod(dir_ids[None] + signs * dir_step[:, freq_ids], NDIR)
    next_dir = jnp.mod(base_dir + 1, NDIR)
    corners = [base_freq * NDIR + base_dir, (base_freq + 1) * NDIR + base_dir, base_freq * NDIR + next_dir, (base_freq + 1) * NDIR + next_dir]
    return jnp.stack(corners, axis=-1).astype(jnp.int32)


def draw_quad_index(key, part):
    return quad_corners(key)


def draw_quad_weight(key, part):
    frac_key = jax.random.fold_in(key, 303)
    fracs = jax.random.uniform(frac_key, (2, NDIR * NFREQ, 2), dtype=jnp.float32)
    along_freq = fracs[..., 0]
    along_dir = fracs[..., 1]
    weights = [(1.0 - along_freq) * (1.0 - along_dir), along_freq * (1.0 - along_dir), (1.0 - along_freq) * along_dir, along_freq * along_dir]
    return jnp.stack(weights, axis=-1).astype(jnp.float32)


def plant(result, stream_key, smallest, largest):
    longest = result.shape.index(max(result.shape))
    spots = []
    for shift in (0, 1):
        where = [jax.random.randint(jax.random.fold_in(stream_key, axis), (), 0, length) for axis, length in enumerate(result.shape)]
        where[longest] = (where[longest] + shift) % result.shape[longest]
        spots.append(tuple(where))
    return result.at[spots[0]].set(smallest).at[spots[1]].set(largest)


def levels(rng, dims, shards, least, largest):
    factor_of, own = 1.0, jax.random.fold_in(rng, 6)
    for dim, parts in shards:
        heights = jnp.exp(jax.random.uniform(jax.random.fold_in(own, dim), (parts,), jnp.float32, least / len(shards), largest / len(shards)))
        factor_of = factor_of * jnp.repeat(heights, dims[dim] // parts).reshape([-1 if axis == dim else 1 for axis in range(len(dims))])
    return factor_of


def setup_inputs(seed: int = 0, part: int = 0) -> dict:
    arg_keys = jax.random.split(jax.random.key(seed), 10)
    part_splits = jax.random.split(jax.random.fold_in(arg_keys[9], part), 10)
    return {
        "spectrum": jnp.clip(2.0 * jax.random.uniform(part_splits[0], (K, NLAT, NLON), jnp.float32) ** levels(part_splits[0], (K, NLAT, NLON), ((0, 4), (1, 2), (2, 2)), -0.2, 0.2), 0.0, 2.0),
        "sea_mask": plant((jax.random.randint(arg_keys[1], (NLAT, NLON), 0, 4) < 3).astype(jnp.int32), jax.random.fold_in(arg_keys[1], 1), 0, 1),
        "depth_class": plant(jax.random.randint(arg_keys[2], (NLAT, NLON), 0, NDEPTH), jax.random.fold_in(arg_keys[2], 1), 0, NDEPTH - 1).astype(jnp.int32),
        "current_class": plant(jax.random.randint(arg_keys[3], (NLAT, NLON), 0, NCUR), jax.random.fold_in(arg_keys[3], 1), 0, NCUR - 1).astype(jnp.int32),
        "speed_table": jnp.clip(jax.random.uniform(arg_keys[4], (NDEPTH, NFREQ), jnp.float32, 0.1, 0.5), 0.1, 0.5),
        "current_table": jnp.clip(jax.random.uniform(arg_keys[5], (NCUR, 2), jnp.float32, -0.14, 0.14), -0.14, 0.14),
        "coupling": jnp.clip(jnp.exp(jax.random.uniform(arg_keys[6], (K,), jnp.float32, math.log(0.05), math.log(0.5))), 0.05, 0.5),
        "quad_index": draw_quad_index(jax.random.fold_in(arg_keys[9], 71), part),
        "quad_weight": draw_quad_weight(jax.random.fold_in(arg_keys[9], 71), part),
    }


plus_factor = 0.4096
minus_factor = 3.160494
cross_factor = 2.007843


def minmod(former, latter):
    return jnp.maximum(0.0, jnp.minimum(former, latter)) + jnp.minimum(0.0, jnp.maximum(former, latter))


def part_of(array, start, length, axis):
    return lax.slice_in_dim(array, start, start + length, axis=axis)


def face_flux(energy, cour, wet_cells, axis):
    length = energy.shape[axis]
    differences = part_of(energy, 1, length - 1, axis) - part_of(energy, 0, length - 1, axis)
    slopes = minmod(part_of(differences, 1, length - 2, axis), part_of(differences, 0, length - 2, axis))
    face_count = length - 3
    face_speed = 0.5 * (part_of(cour, 1, face_count, axis) + part_of(cour, 2, face_count, axis)) * (part_of(wet_cells, 1, face_count, axis) * part_of(wet_cells, 2, face_count, axis))
    upwind_left = part_of(energy, 1, face_count, axis) + 0.5 * (1.0 - face_speed) * part_of(slopes, 0, face_count, axis)
    upwind_right = part_of(energy, 2, face_count, axis) - 0.5 * (1.0 + face_speed) * part_of(slopes, 1, face_count, axis)
    return jnp.maximum(face_speed, 0.0) * upwind_left + jnp.minimum(face_speed, 0.0) * upwind_right


def advance(energy, cour_x, cour_y, wet_cells):
    flux_lon = face_flux(energy[:, 2:-2, :], cour_x[:, 2:-2, :], wet_cells[:, 2:-2, :], 2)
    flux_lat = face_flux(energy[:, :, 2:-2], cour_y[:, :, 2:-2], wet_cells[:, :, 2:-2], 1)
    return energy[:, 2:-2, 2:-2] - (flux_lon[:, :, 1:] - flux_lon[:, :, :-1]) - (flux_lat[:, 1:, :] - flux_lat[:, :-1, :])


def courant(comp_ids, depth_grid, current_grid, speed_table, current_table):
    n_depth, n_freq = speed_table.shape
    n_current = current_table.shape[0]
    depth_hot = (depth_grid[None] == jnp.arange(n_depth, dtype=jnp.int32)[:, None, None]).astype(jnp.float32)
    current_hot = (current_grid[None] == jnp.arange(n_current, dtype=jnp.int32)[:, None, None]).astype(jnp.float32)
    freq_hot = ((comp_ids // NDIR)[:, None] == jnp.arange(n_freq, dtype=jnp.int32)[None, :]).astype(jnp.float32)
    comp_speed = jnp.dot(freq_hot, speed_table.T, precision=lax.Precision.HIGHEST)
    speeds = jnp.einsum("kn,nhw->khw", comp_speed, depth_hot, precision=lax.Precision.HIGHEST)
    current_uv = jnp.einsum("nc,nhw->chw", current_table, current_hot, precision=lax.Precision.HIGHEST)
    angles = (2.0 * math.pi / NDIR) * (comp_ids % NDIR).astype(jnp.float32)
    cour_x = speeds * jnp.cos(angles)[:, None, None] + current_uv[0]
    cour_y = speeds * jnp.sin(angles)[:, None, None] + current_uv[1]
    return cour_x, cour_y


def dense_kernel(table_index, table_weight):
    comp_total = table_index.shape[0]
    columns = jnp.arange(comp_total, dtype=jnp.int32)[None, :]
    weights = table_weight.astype(jnp.bfloat16)
    kernel = jnp.where(columns == table_index[:, 3:4], weights[:, 3:4], jnp.zeros((), jnp.bfloat16))
    for corner in (2, 1, 0):
        kernel = jnp.where(columns == table_index[:, corner:corner + 1], weights[:, corner:corner + 1], kernel)
    return kernel


def interact(energy, kernel_plus, kernel_minus, coupling):
    energy_low = energy.astype(jnp.bfloat16)
    plus_side = jnp.dot(kernel_plus, energy_low, preferred_element_type=jnp.float32)
    minus_side = jnp.dot(kernel_minus, energy_low, preferred_element_type=jnp.float32)
    source = coupling[:, None] * (energy * energy * (plus_factor * plus_side + minus_factor * minus_side) - cross_factor * energy * plus_side * minus_side)
    source_low = source.astype(jnp.bfloat16)
    contract = (((0,), (0,)), ((), ()))
    net_gain = lax.dot_general(kernel_plus, source_low, contract, preferred_element_type=jnp.float32) + lax.dot_general(kernel_minus, source_low, contract, preferred_element_type=jnp.float32) - 2.0 * source
    return energy + net_gain / (1.0 + jnp.abs(net_gain))


def pad_grid(grid_field, rim_width):
    grid_field = jnp.pad(grid_field, ((0, 0), (rim_width, rim_width), (0, 0)))
    return jnp.concatenate([grid_field[:, :, -rim_width:], grid_field, grid_field[:, :, :rim_width]], axis=2)


def reference(spectrum, sea_mask, depth_class, current_class, speed_table, current_table, coupling, quad_index, quad_weight):
    comp_total = NDIR * NFREQ
    wet_cells = sea_mask.astype(jnp.float32)[None]
    wet_pad = pad_grid(wet_cells, 2)
    depth_pad = pad_grid(depth_class[None], 2)[0]
    current_pad = pad_grid(current_class[None], 2)[0]

    def propagate(freq_block):
        comp_ids = freq_block * NDIR + jnp.arange(NDIR, dtype=jnp.int32)
        energy = lax.dynamic_slice_in_dim(spectrum, freq_block * NDIR, NDIR, 0) * wet_cells
        cour_x, cour_y = courant(comp_ids, depth_pad, current_pad, speed_table, current_table)
        for substep in range(SUBSTEPS):
            energy = advance(pad_grid(energy, 2), cour_x, cour_y, wet_pad)
        return energy

    propagated = lax.map(propagate, jnp.arange(NFREQ, dtype=jnp.int32)).reshape(comp_total, NLAT * NLON)
    kernel_plus = dense_kernel(quad_index[0], quad_weight[0])
    kernel_minus = dense_kernel(quad_index[1], quad_weight[1])

    def interact_row(lat_row):
        energy = lax.dynamic_slice_in_dim(propagated, lat_row * NLON, NLON, 1)
        return interact(energy, kernel_plus, kernel_minus, coupling)

    rows_out = lax.map(interact_row, jnp.arange(NLAT, dtype=jnp.int32))
    return jnp.transpose(rows_out, (1, 0, 2))
```

```python
import functools
import math

import jax
import jax.numpy as jnp
import numpy as np
from jax import lax
from jax.experimental import pallas as pl
from jax.experimental.pallas import tpu as pltpu
from jax.sharding import PartitionSpec as P

NDIR = 36
SUBSTEPS = 4


plus_factor = 0.4096
minus_factor = 3.160494
cross_factor = 2.007843


def with_halo(block, sides, width):
    for axis, dim in sides:
        count = lax.axis_size(axis)
        forward = [(i, i + 1) for i in range(count - 1)]
        forward.append((count - 1, 0))
        backward = [(target, source) for source, target in forward]
        low = lax.ppermute(
            lax.slice_in_dim(block, block.shape[dim] - width, None, axis=dim), axis, forward
        )
        high = lax.ppermute(lax.slice_in_dim(block, 0, width, axis=dim), axis, backward)
        block = jnp.concatenate([low, block, high], axis=dim)
    return block


def minmod(former, latter):
    return jnp.maximum(0.0, jnp.minimum(former, latter)) + jnp.minimum(
        0.0, jnp.maximum(former, latter)
    )


def part_of(array, start, length, axis):
    return lax.slice_in_dim(array, start, start + length, axis=axis)


def face_flux(energy, cour, wet_cells, axis):
    length = energy.shape[axis]
    differences = part_of(energy, 1, length - 1, axis) - part_of(energy, 0, length - 1, axis)
    slopes = minmod(
        part_of(differences, 1, length - 2, axis), part_of(differences, 0, length - 2, axis)
    )
    face_count = length - 3
    face_speed = (
        0.5
        * (part_of(cour, 1, face_count, axis) + part_of(cour, 2, face_count, axis))
        * (part_of(wet_cells, 1, face_count, axis) * part_of(wet_cells, 2, face_count, axis))
    )
    upwind_left = part_of(energy, 1, face_count, axis) + 0.5 * (1.0 - face_speed) * part_of(
        slopes, 0, face_count, axis
    )
    upwind_right = part_of(energy, 2, face_count, axis) - 0.5 * (1.0 + face_speed) * part_of(
        slopes, 1, face_count, axis
    )
    return jnp.maximum(face_speed, 0.0) * upwind_left + jnp.minimum(face_speed, 0.0) * upwind_right


def advance(energy, cour_x, cour_y, wet_cells):
    flux_lon = face_flux(energy[:, 2:-2, :], cour_x[:, 2:-2, :], wet_cells[:, 2:-2, :], 2)
    flux_lat = face_flux(energy[:, :, 2:-2], cour_y[:, :, 2:-2], wet_cells[:, :, 2:-2], 1)
    return (
        energy[:, 2:-2, 2:-2]
        - (flux_lon[:, :, 1:] - flux_lon[:, :, :-1])
        - (flux_lat[:, 1:, :] - flux_lat[:, :-1, :])
    )


def courant(comp_ids, depth_grid, current_grid, speed_table, current_table):
    n_depth, n_freq = speed_table.shape
    n_current = current_table.shape[0]
    depth_hot = (depth_grid[None] == jnp.arange(n_depth, dtype=jnp.int32)[:, None, None]).astype(
        jnp.float32
    )
    current_hot = (
        current_grid[None] == jnp.arange(n_current, dtype=jnp.int32)[:, None, None]
    ).astype(jnp.float32)
    freq_hot = ((comp_ids // NDIR)[:, None] == jnp.arange(n_freq, dtype=jnp.int32)[None, :]).astype(
        jnp.float32
    )
    comp_speed = jnp.dot(freq_hot, speed_table.T, precision=lax.Precision.HIGHEST)
    speeds = jnp.einsum("kn,nhw->khw", comp_speed, depth_hot, precision=lax.Precision.HIGHEST)
    current_uv = jnp.einsum(
        "nc,nhw->chw", current_table, current_hot, precision=lax.Precision.HIGHEST
    )
    angles = 2.0 * math.pi / NDIR * (comp_ids % NDIR).astype(jnp.float32)
    cour_x = speeds * jnp.cos(angles)[:, None, None] + current_uv[0]
    cour_y = speeds * jnp.sin(angles)[:, None, None] + current_uv[1]
    return (cour_x, cour_y)


def dense_kernel(table_index, table_weight):
    comp_total = table_index.shape[0]
    columns = jnp.arange(comp_total, dtype=jnp.int32)[None, :]
    weights = table_weight.astype(jnp.bfloat16)
    kernel = jnp.where(columns == table_index[:, 3:4], weights[:, 3:4], jnp.zeros((), jnp.bfloat16))
    for corner in (2, 1, 0):
        kernel = jnp.where(
            columns == table_index[:, corner : corner + 1], weights[:, corner : corner + 1], kernel
        )
    return kernel


def interact(energy, kernel_plus, kernel_minus, coupling):
    energy_low = energy.astype(jnp.bfloat16)
    plus_side = jnp.dot(kernel_plus, energy_low, preferred_element_type=jnp.float32)
    minus_side = jnp.dot(kernel_minus, energy_low, preferred_element_type=jnp.float32)
    source = coupling[:, None] * (
        energy * energy * (plus_factor * plus_side + minus_factor * minus_side)
        - cross_factor * energy * plus_side * minus_side
    )
    source_low = source.astype(jnp.bfloat16)
    contract = (((0,), (0,)), ((), ()))
    net_gain = (
        lax.dot_general(kernel_plus, source_low, contract, preferred_element_type=jnp.float32)
        + lax.dot_general(kernel_minus, source_low, contract, preferred_element_type=jnp.float32)
        - 2.0 * source
    )
    return energy + net_gain / (1.0 + jnp.abs(net_gain))


def window(array, offset):
    return array[:, offset : array.shape[1] - offset, offset : array.shape[2] - offset]


def local(
    spectrum,
    sea_mask,
    depth_class,
    current_class,
    speed_table,
    current_table,
    coupling,
    quad_index,
    quad_weight,
):
    comps_local, lat_rows, lon_cols = spectrum.shape
    n_comp = lax.axis_size("comp")
    n_lat = lax.axis_size("lat")
    deep_rim = 2 * SUBSTEPS
    stacked = jnp.stack([sea_mask, depth_class, current_class])
    padded = with_halo(stacked, (("lat", 1), ("lon", 2)), deep_rim)
    row_global = (
        lax.axis_index("lat") * lat_rows
        - deep_rim
        + jnp.arange(lat_rows + 2 * deep_rim, dtype=jnp.int32)
    )
    inside = ((row_global >= 0) & (row_global < lat_rows * n_lat)).astype(jnp.float32)[:, None]
    wet_rim = (padded[0].astype(jnp.float32) * inside)[None]
    comp_ids = lax.axis_index("comp") * comps_local + jnp.arange(comps_local, dtype=jnp.int32)
    cour_x, cour_y = courant(comp_ids, padded[1], padded[2], speed_table, current_table)
    energy = spectrum * sea_mask.astype(jnp.float32)[None]
    inner_rows = inside[deep_rim - 2 : deep_rim + lat_rows + 2]
    offset = deep_rim - 2
    for substep in range(SUBSTEPS):
        rimmed = with_halo(energy, (("lat", 1), ("lon", 2)), 2) * inner_rows[None]
        energy = advance(
            rimmed, window(cour_x, offset), window(cour_y, offset), window(wet_rim, offset)
        )
    kernel_plus = dense_kernel(quad_index[0], quad_weight[0])
    kernel_minus = dense_kernel(quad_index[1], quad_weight[1])
    cell_count = lat_rows * lon_cols
    outgoing = energy.reshape(comps_local, n_comp, cell_count // n_comp)
    pieces = lax.all_to_all(outgoing, "comp", split_axis=1, concat_axis=0, tiled=True)
    point_grid = pieces.reshape(pieces.shape[0], pieces.shape[2])
    arrived = interact(point_grid, kernel_plus, kernel_minus, coupling).reshape(pieces.shape)
    returned = lax.all_to_all(arrived, "comp", split_axis=0, concat_axis=1, tiled=True)
    return returned.reshape(comps_local, lat_rows, lon_cols)


CHUNK = 24
BLOCK = 4
TILE = 128
MESH = pl.DeviceIdType.MESH


def limited(upper, lower):
    return jnp.maximum(
        jnp.minimum(upper, lower), jnp.minimum(jnp.maximum(upper, lower), 0.0)
    )


def aligned(index, unit):
    return pl.multiple_of(index, unit)


def step_kernel(
    nz,
    nx,
    nc,
    spec,
    grids,
    coupling,
    qi_cols,
    qw_cols,
    qi_rows,
    qw_rows,
    speed_table,
    current_table,
    turns,
    out,
    gbuf,
    buf,
    fields,
    base,
    send,
    arrived,
    low,
    kern,
    kern_t,
    source,
    source_low,
    result,
    returned,
    sem_grid_s,
    sem_grid_r,
    sem_a_s,
    sem_a_r,
    sem_c_s,
    sem_c_r,
    sem_d_s,
    sem_d_r,
):
    z, x, c = lax.axis_index("comp"), lax.axis_index("lat"), lax.axis_index("lon")
    group = nx * nc
    me = x * nc + c
    rows, cols = returned.shape[0], returned.shape[2]
    comps_local = returned.shape[1]
    comps_own = buf.shape[1] // rows
    comp_total = arrived.shape[1]
    row_share = rows // nz
    chunks = comps_own // CHUNK
    all_rows, all_cols = rows * nx, cols * nc

    def place(dz, dg):
        other = lax.rem(me + dg, group)
        return lax.rem(z + dz, nz), other, {
            "comp": lax.rem(z + dz, nz),
            "lat": other // nc,
            "lon": lax.rem(other, nc),
        }

    barrier = pltpu.get_barrier_semaphore()
    for dz in range(nz):
        for dg in range(group):
            if dz or dg:
                _, _, there = place(dz, dg)
                pl.semaphore_signal(barrier, inc=1, device_id=there, device_id_type=MESH)
    pl.semaphore_wait(barrier, nz * group - 1)

    pltpu.make_async_copy(grids, gbuf.at[me], sem_grid_r.at[me]).start()
    for dg in range(1, group):
        _, other, there = place(0, dg)
        pltpu.make_async_remote_copy(
            src_ref=grids,
            dst_ref=gbuf.at[me],
            send_sem=sem_grid_s.at[dg],
            recv_sem=sem_grid_r.at[me],
            device_id=there,
            device_id_type=MESH,
        ).start()
    span = CHUNK * rows

    @pl.loop(0, chunks)
    def _(ch):
        here = pl.ds(aligned(ch * span, span), span)
        for dg in range(group):
            _, other, there = place(0, dg)
            taken = pl.ds(aligned(other * (comps_own * rows) + ch * span, span), span)
            if dg == 0:
                pltpu.make_async_copy(
                    spec.at[taken], buf.at[me, here], sem_a_r.at[me, ch]
                ).start()
            else:
                pltpu.make_async_remote_copy(
                    src_ref=spec.at[taken],
                    dst_ref=buf.at[me, here],
                    send_sem=sem_a_s.at[dg, ch],
                    recv_sem=sem_a_r.at[me, ch],
                    device_id=there,
                    device_id_type=MESH,
                ).start()

    lanes = lax.broadcasted_iota(jnp.int32, (TILE, comp_total), 1)
    subs = lax.broadcasted_iota(jnp.int32, (TILE, comp_total), 0)

    def make_dense(t):
        start = aligned(t * TILE, TILE)
        spot = pl.ds(start, TILE)
        for side in range(2):
            block = jnp.zeros((TILE, comp_total), jnp.float32)
            for corner in range(4):
                col = side * 4 + corner
                block = jnp.where(
                    lanes == qi_cols[spot, col : col + 1], qw_cols[spot, col : col + 1], block
                )
            kern[side, spot, :] = block.astype(jnp.bfloat16)

    def make_dense_t(t):
        start = aligned(t * TILE, TILE)
        spot = pl.ds(start, TILE)
        both = []
        for side in range(2):
            block = jnp.zeros((TILE, comp_total), jnp.float32)
            for corner in range(4):
                row = side * 4 + corner
                block = jnp.where(
                    subs + start == qi_rows[row : row + 1, :], qw_rows[row : row + 1, :], block
                )
            both.append(block)
        kern_t[spot, :] = (both[0] + both[1]).astype(jnp.bfloat16)

    for g in range(group):
        pltpu.make_async_copy(gbuf.at[g], gbuf.at[g], sem_grid_r.at[g]).wait()

    def whole(pick):
        return jnp.concatenate(
            [
                jnp.concatenate([pick(i * nc + j) for j in range(nc)], axis=1)
                for i in range(nx)
            ],
            axis=0,
        )

    row_ids = lax.broadcasted_iota(jnp.int32, (all_rows, all_cols), 0)

    def east(v):
        return pltpu.roll(v, all_cols - 1, 1)

    def west(v):
        return pltpu.roll(v, 1, 1)

    def north(v):
        return jnp.where(row_ids < all_rows - 1, pltpu.roll(v, all_rows - 1, 0), 0.0)

    def south(v):
        return jnp.where(row_ids > 0, pltpu.roll(v, 1, 0), 0.0)

    wet = whole(lambda g: gbuf[g, 0]).astype(jnp.float32)
    depth = whole(lambda g: gbuf[g, 1])
    current = whole(lambda g: gbuf[g, 2])
    wet_x = 0.5 * (wet * east(wet))
    wet_y = 0.5 * (wet * north(wet))
    flow_x = jnp.zeros_like(wet)
    flow_y = jnp.zeros_like(wet)
    for n in range(current_table.shape[0]):
        flow_x = jnp.where(current == n, current_table[n, 0], flow_x)
        flow_y = jnp.where(current == n, current_table[n, 1], flow_y)
    base[0] = (flow_x + east(flow_x)) * wet_x
    base[1] = (flow_y + north(flow_y)) * wet_y
    base[2] = wet
    first_freq = (z * comps_local + me * comps_own) // NDIR
    for j in range(comps_own // NDIR):
        speed = jnp.zeros_like(wet)
        for n in range(speed_table.shape[0]):
            speed = jnp.where(depth == n, speed_table[n, first_freq + j], speed)
        fields[j, 0] = (speed + east(speed)) * wet_x
        fields[j, 1] = (speed + north(speed)) * wet_y

    def propagate(first):
        freq = first // NDIR
        angle = lax.rem(first, NDIR)
        for k in range(BLOCK):
            spot = pl.ds(aligned((first + k) * rows, rows), rows)
            energy = whole(lambda g: buf[g, spot, :]) * base[2]
            speed_x = fields[freq, 0] * turns[0, angle + k] + base[0]
            speed_y = fields[freq, 1] * turns[1, angle + k] + base[1]
            size_x, size_y = jnp.abs(speed_x), jnp.abs(speed_y)
            half_x = 0.5 * size_x * (1.0 - size_x)
            half_y = 0.5 * size_y * (1.0 - size_y)
            for _ in range(SUBSTEPS):
                ahead, behind = east(energy), west(energy)
                slope = limited(ahead - energy, energy - behind)
                flux_x = speed_x * jnp.where(speed_x > 0.0, energy, ahead) + half_x * jnp.where(
                    speed_x > 0.0, slope, east(slope)
                )
                ahead, behind = north(energy), south(energy)
                slope = limited(ahead - energy, energy - behind)
                flux_y = speed_y * jnp.where(speed_y > 0.0, energy, ahead) + half_y * jnp.where(
                    speed_y > 0.0, slope, pltpu.roll(slope, all_rows - 1, 0)
                )
                energy = (
                    energy - (flux_x - west(flux_x)) - (flux_y - pltpu.roll(flux_y, 1, 0))
                )
            for i in range(nx):
                for j in range(nc):
                    buf[i * nc + j, spot, :] = energy[
                        i * rows : (i + 1) * rows, j * cols : (j + 1) * cols
                    ]

    own_first = (z * group + me) * comps_own

    def pass_on(row, start, count, sem_row):
        there_spot = pl.ds(aligned(own_first + start, 8), count)
        here_spot = pl.ds(aligned(start, 8), count)
        for dz in (2, 1, 3, 0) if nz == 4 else range(nz):
            for dg in range(group):
                to_z, other, there = place(dz, dg)
                piece = send.at[other, to_z * row_share + row, here_spot]
                target = arrived.at[row, there_spot]
                if dz or dg:
                    pltpu.make_async_remote_copy(
                        src_ref=piece,
                        dst_ref=target,
                        send_sem=sem_c_s.at[row],
                        recv_sem=sem_c_r.at[row],
                        device_id=there,
                        device_id_type=MESH,
                    ).start()
                else:
                    pltpu.make_async_copy(piece, target, sem_c_r.at[row]).start()

    @pl.loop(0, chunks)
    def _(ch):
        here = pl.ds(aligned(ch * span, span), span)
        for g in range(group):
            pltpu.make_async_copy(
                buf.at[g, here], buf.at[g, here], sem_a_r.at[g, ch]
            ).wait()

        @pl.loop(0, CHUNK // BLOCK)
        def _(b):
            propagate(ch * CHUNK + b * BLOCK)

        for g in range(group):
            for row in range(rows):
                send[g, row, pl.ds(aligned(ch * CHUNK, 8), CHUNK), :] = buf[
                    g, pl.ds(ch * span + row, CHUNK, stride=rows), :
                ]
        pass_on(0, ch * CHUNK, CHUNK, 0)

    for row in range(1, row_share):
        pass_on(row, 0, comps_own, row)

    pl.loop(0, comp_total // TILE)(make_dense)
    pl.loop(0, comp_total // TILE)(make_dense_t)

    for row in range(row_share):
        pltpu.make_async_copy(arrived.at[row], arrived.at[row], sem_c_r.at[row]).wait()
        low[...] = arrived[row].astype(jnp.bfloat16)

        @pl.loop(0, comp_total // TILE)
        def _(t):
            spot = pl.ds(aligned(t * TILE, TILE), TILE)
            plus = jnp.dot(kern[0, spot, :], low[...], preferred_element_type=jnp.float32)
            minus = jnp.dot(kern[1, spot, :], low[...], preferred_element_type=jnp.float32)
            energy = arrived[row, spot, :]
            gain = coupling[spot, :] * (
                energy * energy * (plus_factor * plus + minus_factor * minus)
                - cross_factor * energy * plus * minus
            )
            source[spot, :] = gain
            source_low[spot, :] = gain.astype(jnp.bfloat16)

        for dz in (2, 1, 3, 0) if nz == 4 else range(nz):
            to_z, _, there = place(dz, 0)
            first = to_z * comps_local

            @pl.loop(0, comps_local // 96)
            def _(t):
                spot = pl.ds(aligned(first + t * 96, 32), 96)
                net = (
                    jnp.dot(kern_t[spot, :], source_low[...], preferred_element_type=jnp.float32)
                    - 2.0 * source[spot, :]
                )
                result[row, spot, :] = arrived[row, spot, :] + net / (1.0 + jnp.abs(net))

            piece = result.at[row, pl.ds(aligned(first, 8), comps_local)]
            target = returned.at[z * row_share + row]
            if dz:
                pltpu.make_async_remote_copy(
                    src_ref=piece,
                    dst_ref=target,
                    send_sem=sem_d_s.at[row],
                    recv_sem=sem_d_r.at[row],
                    device_id=there,
                    device_id_type=MESH,
                ).start()
            else:
                pltpu.make_async_copy(piece, target, sem_d_r.at[row]).start()

    for row in range(row_share):
        all_z = returned.at[pl.ds(0, nz)]
        pltpu.make_async_copy(all_z, all_z, sem_d_r.at[row]).wait()
        for quarter in range(nz):
            line = quarter * row_share + row
            out[pl.ds(line, comps_local, stride=rows), :] = returned[line]

    for dg in range(1, group):
        pltpu.make_async_copy(grids, gbuf.at[0], sem_grid_s.at[dg]).wait()

        @pl.loop(0, chunks)
        def _(ch):
            here = pl.ds(0, span)
            pltpu.make_async_copy(buf.at[0, here], buf.at[0, here], sem_a_s.at[dg, ch]).wait()

    for row in range(row_share):
        sent = arrived.at[row, pl.ds(0, comp_total - comps_own)]
        pltpu.make_async_copy(sent, sent, sem_c_s.at[row]).wait()
        sent = returned.at[pl.ds(0, nz - 1)]
        pltpu.make_async_copy(sent, sent, sem_d_s.at[row]).wait()


def fused(nz, nx, nc, *arrays):
    (
        spectrum,
        sea_mask,
        depth_class,
        current_class,
        speed_table,
        current_table,
        coupling,
        quad_index,
        quad_weight,
    ) = arrays
    comps_local, rows, cols = spectrum.shape
    comp_total = coupling.shape[0]
    group = nx * nc
    own = comps_local // group
    share = rows // nz
    turn = 2.0 * math.pi / NDIR * np.arange(NDIR)
    turns = jnp.asarray(np.stack([np.cos(turn), np.sin(turn)]), jnp.float32)
    vmem = pl.BlockSpec(memory_space=pltpu.VMEM)
    smem = pl.BlockSpec(memory_space=pltpu.SMEM)
    f32, bf16, i32 = jnp.float32, jnp.bfloat16, jnp.int32
    dma = pltpu.SemaphoreType.DMA
    qi_rows = quad_index.transpose(0, 2, 1).reshape(8, comp_total)
    qw_rows = quad_weight.transpose(0, 2, 1).reshape(8, comp_total)
    out = pl.pallas_call(
        functools.partial(step_kernel, nz, nx, nc),
        name="wave_step",
        out_shape=jax.ShapeDtypeStruct((comps_local * rows, cols), f32),
        in_specs=[pl.BlockSpec(memory_space=pl.ANY)] + [vmem] * 6 + [smem] * 3,
        out_specs=vmem,
        scratch_shapes=[
            pltpu.VMEM((group, 3, rows, cols), i32),
            pltpu.VMEM((group, own * rows, cols), f32),
            pltpu.VMEM((own // NDIR, 2, rows * nx, cols * nc), f32),
            pltpu.VMEM((3, rows * nx, cols * nc), f32),
            pltpu.VMEM((group, rows, own, cols), f32),
            pltpu.VMEM((share, comp_total, cols), f32),
            pltpu.VMEM((comp_total, cols), bf16),
            pltpu.VMEM((2, comp_total, comp_total), bf16),
            pltpu.VMEM((comp_total, comp_total), bf16),
            pltpu.VMEM((comp_total, cols), f32),
            pltpu.VMEM((comp_total, cols), bf16),
            pltpu.VMEM((share, comp_total, cols), f32),
            pltpu.VMEM((rows, comps_local, cols), f32),
            dma((group,)),
            dma((group,)),
            dma((group, own // CHUNK)),
            dma((group, own // CHUNK)),
            dma((share,)),
            dma((share,)),
            dma((share,)),
            dma((share,)),
        ],
        compiler_params=pltpu.CompilerParams(
            collective_id=0, has_side_effects=True, vmem_limit_bytes=60 * 1024 * 1024
        ),
    )(
        spectrum.reshape(comps_local * rows, cols),
        jnp.stack([sea_mask, depth_class, current_class]),
        coupling[:, None],
        qi_rows.T,
        qw_rows.T,
        qi_rows,
        qw_rows,
        speed_table,
        current_table,
        turns,
    )
    return out.reshape(comps_local, rows, cols)


def step(*arrays):
    comps_local, rows, cols = arrays[0].shape
    comp_total = arrays[6].shape[0]
    nz, nx, nc = (lax.axis_size(a) for a in ("comp", "lat", "lon"))
    own = comps_local // (nx * nc)
    fits = (
        comps_local % (nx * nc) == 0
        and own % NDIR == 0
        and own % CHUNK == 0
        and NDIR % BLOCK == 0
        and rows == 8
        and cols % 128 == 0
        and rows % nz == 0
        and comp_total % TILE == 0
        and comps_local % 96 == 0
    )
    return fused(nz, nx, nc, *arrays) if fits else local(*arrays)


def solution(mesh):
    placed = (
        P(("ens", "comp"), "lat", "lon"),
        P("lat", "lon"),
        P("lat", "lon"),
        P("lat", "lon"),
        P(),
        P(),
        P(),
        P(),
        P(),
    )
    return jax.shard_map(
        step,
        mesh=mesh,
        in_specs=placed,
        out_specs=P(("ens", "comp"), "lat", "lon"),
        check_vma=False,
    )
```

```python
import functools
import math

import jax
import jax.numpy as jnp
import numpy as np
from jax import lax
from jax.experimental import pallas as pl
from jax.experimental.pallas import tpu as pltpu
from jax.sharding import PartitionSpec as P

NDIR = 36
SUBSTEPS = 4


plus_factor = 0.4096
minus_factor = 3.160494
cross_factor = 2.007843


def with_halo(block, sides, width):
    for axis, dim in sides:
        count = lax.axis_size(axis)
        forward = [(i, i + 1) for i in range(count - 1)]
        forward.append((count - 1, 0))
        backward = [(target, source) for source, target in forward]
        low = lax.ppermute(
            lax.slice_in_dim(block, block.shape[dim] - width, None, axis=dim), axis, forward
        )
        high = lax.ppermute(lax.slice_in_dim(block, 0, width, axis=dim), axis, backward)
        block = jnp.concatenate([low, block, high], axis=dim)
    return block


def minmod(former, latter):
    return jnp.maximum(0.0, jnp.minimum(former, latter)) + jnp.minimum(
        0.0, jnp.maximum(former, latter)
    )


def part_of(array, start, length, axis):
    return lax.slice_in_dim(array, start, start + length, axis=axis)


def face_flux(energy, cour, wet_cells, axis):
    length = energy.shape[axis]
    differences = part_of(energy, 1, length - 1, axis) - part_of(energy, 0, length - 1, axis)
    slopes = minmod(
        part_of(differences, 1, length - 2, axis), part_of(differences, 0, length - 2, axis)
    )
    face_count = length - 3
    face_speed = (
        0.5
        * (part_of(cour, 1, face_count, axis) + part_of(cour, 2, face_count, axis))
        * (part_of(wet_cells, 1, face_count, axis) * part_of(wet_cells, 2, face_count, axis))
    )
    upwind_left = part_of(energy, 1, face_count, axis) + 0.5 * (1.0 - face_speed) * part_of(
        slopes, 0, face_count, axis
    )
    upwind_right = part_of(energy, 2, face_count, axis) - 0.5 * (1.0 + face_speed) * part_of(
        slopes, 1, face_count, axis
    )
    return jnp.maximum(face_speed, 0.0) * upwind_left + jnp.minimum(face_speed, 0.0) * upwind_right


def advance(energy, cour_x, cour_y, wet_cells):
    flux_lon = face_flux(energy[:, 2:-2, :], cour_x[:, 2:-2, :], wet_cells[:, 2:-2, :], 2)
    flux_lat = face_flux(energy[:, :, 2:-2], cour_y[:, :, 2:-2], wet_cells[:, :, 2:-2], 1)
    return (
        energy[:, 2:-2, 2:-2]
        - (flux_lon[:, :, 1:] - flux_lon[:, :, :-1])
        - (flux_lat[:, 1:, :] - flux_lat[:, :-1, :])
    )


def courant(comp_ids, depth_grid, current_grid, speed_table, current_table):
    n_depth, n_freq = speed_table.shape
    n_current = current_table.shape[0]
    depth_hot = (depth_grid[None] == jnp.arange(n_depth, dtype=jnp.int32)[:, None, None]).astype(
        jnp.float32
    )
    current_hot = (
        current_grid[None] == jnp.arange(n_current, dtype=jnp.int32)[:, None, None]
    ).astype(jnp.float32)
    freq_hot = ((comp_ids // NDIR)[:, None] == jnp.arange(n_freq, dtype=jnp.int32)[None, :]).astype(
        jnp.float32
    )
    comp_speed = jnp.dot(freq_hot, speed_table.T, precision=lax.Precision.HIGHEST)
    speeds = jnp.einsum("kn,nhw->khw", comp_speed, depth_hot, precision=lax.Precision.HIGHEST)
    current_uv = jnp.einsum(
        "nc,nhw->chw", current_table, current_hot, precision=lax.Precision.HIGHEST
    )
    angles = 2.0 * math.pi / NDIR * (comp_ids % NDIR).astype(jnp.float32)
    cour_x = speeds * jnp.cos(angles)[:, None, None] + current_uv[0]
    cour_y = speeds * jnp.sin(angles)[:, None, None] + current_uv[1]
    return (cour_x, cour_y)


def dense_kernel(table_index, table_weight):
    comp_total = table_index.shape[0]
    columns = jnp.arange(comp_total, dtype=jnp.int32)[None, :]
    weights = table_weight.astype(jnp.bfloat16)
    kernel = jnp.where(columns == table_index[:, 3:4], weights[:, 3:4], jnp.zeros((), jnp.bfloat16))
    for corner in (2, 1, 0):
        kernel = jnp.where(
            columns == table_index[:, corner : corner + 1], weights[:, corner : corner + 1], kernel
        )
    return kernel


def interact(energy, kernel_plus, kernel_minus, coupling):
    energy_low = energy.astype(jnp.bfloat16)
    plus_side = jnp.dot(kernel_plus, energy_low, preferred_element_type=jnp.float32)
    minus_side = jnp.dot(kernel_minus, energy_low, preferred_element_type=jnp.float32)
    source = coupling[:, None] * (
        energy * energy * (plus_factor * plus_side + minus_factor * minus_side)
        - cross_factor * energy * plus_side * minus_side
    )
    source_low = source.astype(jnp.bfloat16)
    contract = (((0,), (0,)), ((), ()))
    net_gain = (
        lax.dot_general(kernel_plus, source_low, contract, preferred_element_type=jnp.float32)
        + lax.dot_general(kernel_minus, source_low, contract, preferred_element_type=jnp.float32)
        - 2.0 * source
    )
    return energy + net_gain / (1.0 + jnp.abs(net_gain))


def window(array, offset):
    return array[:, offset : array.shape[1] - offset, offset : array.shape[2] - offset]


def local(
    spectrum,
    sea_mask,
    depth_class,
    current_class,
    speed_table,
    current_table,
    coupling,
    quad_index,
    quad_weight,
):
    comps_local, lat_rows, lon_cols = spectrum.shape
    n_comp = lax.axis_size("comp")
    n_lat = lax.axis_size("lat")
    deep_rim = 2 * SUBSTEPS
    stacked = jnp.stack([sea_mask, depth_class, current_class])
    padded = with_halo(stacked, (("lat", 1), ("lon", 2)), deep_rim)
    row_global = (
        lax.axis_index("lat") * lat_rows
        - deep_rim
        + jnp.arange(lat_rows + 2 * deep_rim, dtype=jnp.int32)
    )
    inside = ((row_global >= 0) & (row_global < lat_rows * n_lat)).astype(jnp.float32)[:, None]
    wet_rim = (padded[0].astype(jnp.float32) * inside)[None]
    comp_ids = lax.axis_index("comp") * comps_local + jnp.arange(comps_local, dtype=jnp.int32)
    cour_x, cour_y = courant(comp_ids, padded[1], padded[2], speed_table, current_table)
    energy = spectrum * sea_mask.astype(jnp.float32)[None]
    inner_rows = inside[deep_rim - 2 : deep_rim + lat_rows + 2]
    offset = deep_rim - 2
    for substep in range(SUBSTEPS):
        rimmed = with_halo(energy, (("lat", 1), ("lon", 2)), 2) * inner_rows[None]
        energy = advance(
            rimmed, window(cour_x, offset), window(cour_y, offset), window(wet_rim, offset)
        )
    kernel_plus = dense_kernel(quad_index[0], quad_weight[0])
    kernel_minus = dense_kernel(quad_index[1], quad_weight[1])
    cell_count = lat_rows * lon_cols
    outgoing = energy.reshape(comps_local, n_comp, cell_count // n_comp)
    pieces = lax.all_to_all(outgoing, "comp", split_axis=1, concat_axis=0, tiled=True)
    point_grid = pieces.reshape(pieces.shape[0], pieces.shape[2])
    arrived = interact(point_grid, kernel_plus, kernel_minus, coupling).reshape(pieces.shape)
    returned = lax.all_to_all(arrived, "comp", split_axis=0, concat_axis=1, tiled=True)
    return returned.reshape(comps_local, lat_rows, lon_cols)


CHUNK = 24
BLOCK = 12
TILE = 128
MESH = pl.DeviceIdType.MESH


def limited(upper, lower):
    return jnp.maximum(
        jnp.minimum(upper, lower), jnp.minimum(jnp.maximum(upper, lower), 0.0)
    )


def aligned(index, unit):
    return pl.multiple_of(index, unit)


def step_kernel(
    nz,
    nx,
    nc,
    spec,
    sea_mask,
    depth_class,
    current_class,
    coupling,
    quad_index,
    quad_weight,
    speed_table,
    current_table,
    turns,
    out,
    gbuf,
    buf,
    fields,
    base,
    send,
    arrived,
    low,
    kern,
    kern_t,
    strength,
    source,
    source_low,
    result,
    returned,
    sem_grid_s,
    sem_grid_r,
    sem_a_s,
    sem_a_r,
    sem_c_s,
    sem_c_r,
    sem_d_s,
    sem_d_r,
):
    z, x, c = lax.axis_index("comp"), lax.axis_index("lat"), lax.axis_index("lon")
    group = nx * nc
    me = x * nc + c
    rows, cols = returned.shape[0], returned.shape[2]
    comps_local = returned.shape[1]
    comps_own = buf.shape[1] // rows
    comp_total = arrived.shape[1]
    row_share = rows // nz
    chunks = comps_own // CHUNK
    all_rows, all_cols = rows * nx, cols * nc

    def place(dz, dg):
        other = lax.rem(me + dg, group)
        return lax.rem(z + dz, nz), other, {
            "comp": lax.rem(z + dz, nz),
            "lat": other // nc,
            "lon": lax.rem(other, nc),
        }

    barrier = pltpu.get_barrier_semaphore()
    for dz in range(nz):
        for dg in range(group):
            if dz or dg:
                _, _, there = place(dz, dg)
                pl.semaphore_signal(barrier, inc=1, device_id=there, device_id_type=MESH)
    pl.semaphore_wait(barrier, nz * group - 1)

    for i, grid in enumerate((sea_mask, depth_class, current_class)):
        pltpu.make_async_copy(grid, gbuf.at[me, i], sem_grid_r.at[me, i]).start()
        for dg in range(1, group):
            _, other, there = place(0, dg)
            pltpu.make_async_remote_copy(
                src_ref=grid,
                dst_ref=gbuf.at[me, i],
                send_sem=sem_grid_s.at[dg, i],
                recv_sem=sem_grid_r.at[me, i],
                device_id=there,
                device_id_type=MESH,
            ).start()
    span = CHUNK * rows

    @pl.loop(0, chunks)
    def _(ch):
        here = pl.ds(aligned(ch * span, span), span)
        for dg in range(group):
            _, other, there = place(0, dg)
            taken = pl.ds(aligned(other * (comps_own * rows) + ch * span, span), span)
            if dg == 0:
                pltpu.make_async_copy(
                    spec.at[taken], buf.at[me, here], sem_a_r.at[me, ch]
                ).start()
            else:
                pltpu.make_async_remote_copy(
                    src_ref=spec.at[taken],
                    dst_ref=buf.at[me, here],
                    send_sem=sem_a_s.at[dg, ch],
                    recv_sem=sem_a_r.at[me, ch],
                    device_id=there,
                    device_id_type=MESH,
                ).start()

    lanes = lax.broadcasted_iota(jnp.int32, (TILE, comp_total), 1)
    subs = lax.broadcasted_iota(jnp.int32, (TILE, comp_total), 0)

    def make_dense(t):
        start = aligned(t * TILE, TILE)
        spot = pl.ds(start, TILE)
        strength[spot, :] = jnp.broadcast_to(coupling[pl.ds(t, 1), :], (cols, TILE)).T
        indices, weights = (
            jnp.concatenate(
                [table[side, :, spot].astype(jnp.float32) for side in range(2)], axis=0
            ).T
            for table in (quad_index, quad_weight)
        )
        indices = indices.astype(jnp.int32)
        for side in range(2):
            block = jnp.zeros((TILE, comp_total), jnp.float32)
            for corner in range(4):
                col = side * 4 + corner
                block = jnp.where(
                    lanes == indices[:, col : col + 1], weights[:, col : col + 1], block
                )
            kern[side, spot, :] = block.astype(jnp.bfloat16)

    def make_dense_t(t):
        start = aligned(t * TILE, TILE)
        spot = pl.ds(start, TILE)
        both = []
        for side in range(2):
            block = jnp.zeros((TILE, comp_total), jnp.float32)
            for corner in range(4):
                one = slice(corner, corner + 1)
                block = jnp.where(
                    subs + start == quad_index[side, one, :], quad_weight[side, one, :], block
                )
            both.append(block)
        kern_t[spot, :] = (both[0] + both[1]).astype(jnp.bfloat16)

    for g in range(group):
        for i in range(3):
            pltpu.make_async_copy(gbuf.at[g, i], gbuf.at[g, i], sem_grid_r.at[g, i]).wait()

    def whole(pick):
        return jnp.concatenate(
            [
                jnp.concatenate([pick(i * nc + j) for j in range(nc)], axis=1)
                for i in range(nx)
            ],
            axis=0,
        )

    row_ids = lax.broadcasted_iota(jnp.int32, (all_rows, all_cols), 0)

    def east(v):
        return pltpu.roll(v, all_cols - 1, 1)

    def west(v):
        return pltpu.roll(v, 1, 1)

    def north(v):
        return jnp.where(row_ids < all_rows - 1, pltpu.roll(v, all_rows - 1, 0), 0.0)

    def south(v):
        return jnp.where(row_ids > 0, pltpu.roll(v, 1, 0), 0.0)

    wet = whole(lambda g: gbuf[g, 0]).astype(jnp.float32)
    depth = whole(lambda g: gbuf[g, 1])
    current = whole(lambda g: gbuf[g, 2])
    wet_x = 0.5 * (wet * east(wet))
    wet_y = 0.5 * (wet * north(wet))
    flow_x = jnp.zeros_like(wet)
    flow_y = jnp.zeros_like(wet)
    for n in range(current_table.shape[1]):
        flow_x = jnp.where(current == n, current_table[0, n], flow_x)
        flow_y = jnp.where(current == n, current_table[1, n], flow_y)
    base[0] = (flow_x + east(flow_x)) * wet_x
    base[1] = (flow_y + north(flow_y)) * wet_y
    base[2] = wet
    first_freq = (z * comps_local + me * comps_own) // NDIR
    for j in range(comps_own // NDIR):
        speed = jnp.zeros_like(wet)
        for n in range(speed_table.shape[0]):
            speed = jnp.where(depth == n, speed_table[n, first_freq + j], speed)
        fields[j, 0] = (speed + east(speed)) * wet_x
        fields[j, 1] = (speed + north(speed)) * wet_y

    def propagate(first):
        freq = first // NDIR
        angle = lax.rem(first, NDIR)
        for k in range(BLOCK):
            spot = pl.ds(aligned((first + k) * rows, rows), rows)
            energy = whole(lambda g: buf[g, spot, :]) * base[2]
            speed_x = fields[freq, 0] * turns[0, angle + k] + base[0]
            speed_y = fields[freq, 1] * turns[1, angle + k] + base[1]
            size_x, size_y = jnp.abs(speed_x), jnp.abs(speed_y)
            half_x = 0.5 * size_x * (1.0 - size_x)
            half_y = 0.5 * size_y * (1.0 - size_y)
            for _ in range(SUBSTEPS):
                ahead, behind = east(energy), west(energy)
                slope = limited(ahead - energy, energy - behind)
                flux_x = speed_x * jnp.where(speed_x > 0.0, energy, ahead) + half_x * jnp.where(
                    speed_x > 0.0, slope, east(slope)
                )
                ahead, behind = north(energy), south(energy)
                slope = limited(ahead - energy, energy - behind)
                flux_y = speed_y * jnp.where(speed_y > 0.0, energy, ahead) + half_y * jnp.where(
                    speed_y > 0.0, slope, pltpu.roll(slope, all_rows - 1, 0)
                )
                energy = (
                    energy - (flux_x - west(flux_x)) - (flux_y - pltpu.roll(flux_y, 1, 0))
                )
            for i in range(nx):
                for j in range(nc):
                    buf[i * nc + j, spot, :] = energy[
                        i * rows : (i + 1) * rows, j * cols : (j + 1) * cols
                    ]

    own_first = (z * group + me) * comps_own

    def pass_on(row, start, count, sem_row):
        there_spot = pl.ds(aligned(own_first + start, 8), count)
        here_spot = pl.ds(aligned(start, 8), count)
        for dz in (2, 1, 3, 0) if nz == 4 else range(nz):
            for dg in range(group):
                to_z, other, there = place(dz, dg)
                piece = send.at[other, to_z * row_share + row, here_spot]
                target = arrived.at[row, there_spot]
                if dz or dg:
                    pltpu.make_async_remote_copy(
                        src_ref=piece,
                        dst_ref=target,
                        send_sem=sem_c_s.at[row],
                        recv_sem=sem_c_r.at[row],
                        device_id=there,
                        device_id_type=MESH,
                    ).start()
                else:
                    pltpu.make_async_copy(piece, target, sem_c_r.at[row]).start()

    @pl.loop(0, chunks)
    def _(ch):
        here = pl.ds(aligned(ch * span, span), span)
        for g in range(group):
            pltpu.make_async_copy(
                buf.at[g, here], buf.at[g, here], sem_a_r.at[g, ch]
            ).wait()

        @pl.loop(0, CHUNK // BLOCK)
        def _(b):
            propagate(ch * CHUNK + b * BLOCK)

        for g in range(group):
            for row in range(rows):
                send[g, row, pl.ds(aligned(ch * CHUNK, 8), CHUNK), :] = buf[
                    g, pl.ds(ch * span + row, CHUNK, stride=rows), :
                ]
        pass_on(0, ch * CHUNK, CHUNK, 0)

    for row in range(1, row_share):
        pass_on(row, 0, comps_own, row)

    pl.loop(0, comp_total // TILE)(make_dense)
    pl.loop(0, comp_total // TILE)(make_dense_t)

    for row in range(row_share):
        pltpu.make_async_copy(arrived.at[row], arrived.at[row], sem_c_r.at[row]).wait()
        low[...] = arrived[row].astype(jnp.bfloat16)

        @pl.loop(0, comp_total // TILE)
        def _(t):
            spot = pl.ds(aligned(t * TILE, TILE), TILE)
            plus = jnp.dot(kern[0, spot, :], low[...], preferred_element_type=jnp.float32)
            minus = jnp.dot(kern[1, spot, :], low[...], preferred_element_type=jnp.float32)
            energy = arrived[row, spot, :]
            gain = strength[spot, :] * (
                energy * energy * (plus_factor * plus + minus_factor * minus)
                - cross_factor * energy * plus * minus
            )
            source[spot, :] = gain
            source_low[spot, :] = gain.astype(jnp.bfloat16)

        for dz in (2, 1, 3, 0) if nz == 4 else range(nz):
            to_z, _, there = place(dz, 0)
            first = to_z * comps_local

            @pl.loop(0, comps_local // 96)
            def _(t):
                spot = pl.ds(aligned(first + t * 96, 32), 96)
                net = (
                    jnp.dot(kern_t[spot, :], source_low[...], preferred_element_type=jnp.float32)
                    - 2.0 * source[spot, :]
                )
                result[row, spot, :] = arrived[row, spot, :] + net / (1.0 + jnp.abs(net))

            piece = result.at[row, pl.ds(aligned(first, 8), comps_local)]
            target = returned.at[z * row_share + row]
            if dz:
                pltpu.make_async_remote_copy(
                    src_ref=piece,
                    dst_ref=target,
                    send_sem=sem_d_s.at[row],
                    recv_sem=sem_d_r.at[row],
                    device_id=there,
                    device_id_type=MESH,
                ).start()
            else:
                pltpu.make_async_copy(piece, target, sem_d_r.at[row]).start()

    for row in range(row_share):
        all_z = returned.at[pl.ds(0, nz)]
        pltpu.make_async_copy(all_z, all_z, sem_d_r.at[row]).wait()
        for quarter in range(nz):
            line = quarter * row_share + row
            out[pl.ds(line, comps_local, stride=rows), :] = returned[line]

    for dg in range(1, group):
        for i in range(3):
            pltpu.make_async_copy(gbuf.at[0, i], gbuf.at[0, i], sem_grid_s.at[dg, i]).wait()

        @pl.loop(0, chunks)
        def _(ch):
            here = pl.ds(0, span)
            pltpu.make_async_copy(buf.at[0, here], buf.at[0, here], sem_a_s.at[dg, ch]).wait()

    for row in range(row_share):
        sent = arrived.at[row, pl.ds(0, comp_total - comps_own)]
        pltpu.make_async_copy(sent, sent, sem_c_s.at[row]).wait()
        sent = returned.at[pl.ds(0, nz - 1)]
        pltpu.make_async_copy(sent, sent, sem_d_s.at[row]).wait()


def fused(nz, nx, nc, *arrays):
    (
        spectrum,
        sea_mask,
        depth_class,
        current_class,
        speed_table,
        current_table,
        coupling,
        quad_index,
        quad_weight,
    ) = arrays
    comps_local, rows, cols = spectrum.shape
    comp_total = coupling.shape[0]
    group = nx * nc
    own = comps_local // group
    share = rows // nz
    turn = 2.0 * math.pi / NDIR * np.arange(NDIR)
    turns = jnp.asarray(np.stack([np.cos(turn), np.sin(turn)]), jnp.float32)
    vmem = pl.BlockSpec(memory_space=pltpu.VMEM)
    smem = pl.BlockSpec(memory_space=pltpu.SMEM)
    f32, bf16, i32 = jnp.float32, jnp.bfloat16, jnp.int32
    dma = pltpu.SemaphoreType.DMA
    out = pl.pallas_call(
        functools.partial(step_kernel, nz, nx, nc),
        name="wave_step",
        out_shape=jax.ShapeDtypeStruct((comps_local * rows, cols), f32),
        in_specs=[pl.BlockSpec(memory_space=pl.ANY)] + [vmem] * 6 + [smem] * 3,
        out_specs=vmem,
        scratch_shapes=[
            pltpu.VMEM((group, 3, rows, cols), i32),
            pltpu.VMEM((group, own * rows, cols), f32),
            pltpu.VMEM((own // NDIR, 2, rows * nx, cols * nc), f32),
            pltpu.VMEM((3, rows * nx, cols * nc), f32),
            pltpu.VMEM((group, rows, own, cols), f32),
            pltpu.VMEM((share, comp_total, cols), f32),
            pltpu.VMEM((comp_total, cols), bf16),
            pltpu.VMEM((2, comp_total, comp_total), bf16),
            pltpu.VMEM((comp_total, comp_total), bf16),
            pltpu.VMEM((comp_total, cols), f32),
            pltpu.VMEM((comp_total, cols), f32),
            pltpu.VMEM((comp_total, cols), bf16),
            pltpu.VMEM((share, comp_total, cols), f32),
            pltpu.VMEM((rows, comps_local, cols), f32),
            dma((group, 3)),
            dma((group, 3)),
            dma((group, own // CHUNK)),
            dma((group, own // CHUNK)),
            dma((share,)),
            dma((share,)),
            dma((share,)),
            dma((share,)),
        ],
        compiler_params=pltpu.CompilerParams(
            collective_id=0, has_side_effects=True, vmem_limit_bytes=60 * 1024 * 1024
        ),
    )(
        spectrum.reshape(comps_local * rows, cols),
        sea_mask,
        depth_class,
        current_class,
        coupling.reshape(comp_total // TILE, TILE),
        quad_index.transpose(0, 2, 1),
        quad_weight.transpose(0, 2, 1),
        speed_table,
        current_table.T,
        turns,
    )
    return out.reshape(comps_local, rows, cols)


def step(*arrays):
    comps_local, rows, cols = arrays[0].shape
    comp_total = arrays[6].shape[0]
    nz, nx, nc = (lax.axis_size(a) for a in ("comp", "lat", "lon"))
    own = comps_local // (nx * nc)
    fits = (
        comps_local % (nx * nc) == 0
        and own % NDIR == 0
        and own % CHUNK == 0
        and CHUNK % BLOCK == 0
        and NDIR % BLOCK == 0
        and rows == 8
        and cols == TILE
        and rows % nz == 0
        and comp_total % TILE == 0
        and comps_local % 96 == 0
    )
    return fused(nz, nx, nc, *arrays) if fits else local(*arrays)


def solution(mesh):
    placed = (
        P(("ens", "comp"), "lat", "lon"),
        P("lat", "lon"),
        P("lat", "lon"),
        P("lat", "lon"),
        P(),
        P(),
        P(),
        P(),
        P(),
    )
    return jax.shard_map(
        step,
        mesh=mesh,
        in_specs=placed,
        out_specs=P(("ens", "comp"), "lat", "lon"),
        check_vma=False,
    )
```

```python
import functools
import math

import jax
import jax.numpy as jnp
import numpy as np
from jax import lax
from jax.experimental import pallas as pl
from jax.experimental.pallas import tpu as pltpu
from jax.sharding import PartitionSpec as P

NDIR = 36
SUBSTEPS = 4


plus_factor = 0.4096
minus_factor = 3.160494
cross_factor = 2.007843


def with_halo(block, sides, width):
    for axis, dim in sides:
        count = lax.axis_size(axis)
        forward = [(i, i + 1) for i in range(count - 1)]
        forward.append((count - 1, 0))
        backward = [(target, source) for source, target in forward]
        low = lax.ppermute(
            lax.slice_in_dim(block, block.shape[dim] - width, None, axis=dim), axis, forward
        )
        high = lax.ppermute(lax.slice_in_dim(block, 0, width, axis=dim), axis, backward)
        block = jnp.concatenate([low, block, high], axis=dim)
    return block


def minmod(former, latter):
    return jnp.maximum(0.0, jnp.minimum(former, latter)) + jnp.minimum(
        0.0, jnp.maximum(former, latter)
    )


def part_of(array, start, length, axis):
    return lax.slice_in_dim(array, start, start + length, axis=axis)


def face_flux(energy, cour, wet_cells, axis):
    length = energy.shape[axis]
    differences = part_of(energy, 1, length - 1, axis) - part_of(energy, 0, length - 1, axis)
    slopes = minmod(
        part_of(differences, 1, length - 2, axis), part_of(differences, 0, length - 2, axis)
    )
    face_count = length - 3
    face_speed = (
        0.5
        * (part_of(cour, 1, face_count, axis) + part_of(cour, 2, face_count, axis))
        * (part_of(wet_cells, 1, face_count, axis) * part_of(wet_cells, 2, face_count, axis))
    )
    upwind_left = part_of(energy, 1, face_count, axis) + 0.5 * (1.0 - face_speed) * part_of(
        slopes, 0, face_count, axis
    )
    upwind_right = part_of(energy, 2, face_count, axis) - 0.5 * (1.0 + face_speed) * part_of(
        slopes, 1, face_count, axis
    )
    return jnp.maximum(face_speed, 0.0) * upwind_left + jnp.minimum(face_speed, 0.0) * upwind_right


def advance(energy, cour_x, cour_y, wet_cells):
    flux_lon = face_flux(energy[:, 2:-2, :], cour_x[:, 2:-2, :], wet_cells[:, 2:-2, :], 2)
    flux_lat = face_flux(energy[:, :, 2:-2], cour_y[:, :, 2:-2], wet_cells[:, :, 2:-2], 1)
    return (
        energy[:, 2:-2, 2:-2]
        - (flux_lon[:, :, 1:] - flux_lon[:, :, :-1])
        - (flux_lat[:, 1:, :] - flux_lat[:, :-1, :])
    )


def courant(comp_ids, depth_grid, current_grid, speed_table, current_table):
    n_depth, n_freq = speed_table.shape
    n_current = current_table.shape[0]
    depth_hot = (depth_grid[None] == jnp.arange(n_depth, dtype=jnp.int32)[:, None, None]).astype(
        jnp.float32
    )
    current_hot = (
        current_grid[None] == jnp.arange(n_current, dtype=jnp.int32)[:, None, None]
    ).astype(jnp.float32)
    freq_hot = ((comp_ids // NDIR)[:, None] == jnp.arange(n_freq, dtype=jnp.int32)[None, :]).astype(
        jnp.float32
    )
    comp_speed = jnp.dot(freq_hot, speed_table.T, precision=lax.Precision.HIGHEST)
    speeds = jnp.einsum("kn,nhw->khw", comp_speed, depth_hot, precision=lax.Precision.HIGHEST)
    current_uv = jnp.einsum(
        "nc,nhw->chw", current_table, current_hot, precision=lax.Precision.HIGHEST
    )
    angles = 2.0 * math.pi / NDIR * (comp_ids % NDIR).astype(jnp.float32)
    cour_x = speeds * jnp.cos(angles)[:, None, None] + current_uv[0]
    cour_y = speeds * jnp.sin(angles)[:, None, None] + current_uv[1]
    return (cour_x, cour_y)


def dense_kernel(table_index, table_weight):
    comp_total = table_index.shape[0]
    columns = jnp.arange(comp_total, dtype=jnp.int32)[None, :]
    weights = table_weight.astype(jnp.bfloat16)
    kernel = jnp.where(columns == table_index[:, 3:4], weights[:, 3:4], jnp.zeros((), jnp.bfloat16))
    for corner in (2, 1, 0):
        kernel = jnp.where(
            columns == table_index[:, corner : corner + 1], weights[:, corner : corner + 1], kernel
        )
    return kernel


def interact(energy, kernel_plus, kernel_minus, coupling):
    energy_low = energy.astype(jnp.bfloat16)
    plus_side = jnp.dot(kernel_plus, energy_low, preferred_element_type=jnp.float32)
    minus_side = jnp.dot(kernel_minus, energy_low, preferred_element_type=jnp.float32)
    source = coupling[:, None] * (
        energy * energy * (plus_factor * plus_side + minus_factor * minus_side)
        - cross_factor * energy * plus_side * minus_side
    )
    source_low = source.astype(jnp.bfloat16)
    contract = (((0,), (0,)), ((), ()))
    net_gain = (
        lax.dot_general(kernel_plus, source_low, contract, preferred_element_type=jnp.float32)
        + lax.dot_general(kernel_minus, source_low, contract, preferred_element_type=jnp.float32)
        - 2.0 * source
    )
    return energy + net_gain / (1.0 + jnp.abs(net_gain))


def window(array, offset):
    return array[:, offset : array.shape[1] - offset, offset : array.shape[2] - offset]


def local(
    spectrum,
    sea_mask,
    depth_class,
    current_class,
    speed_table,
    current_table,
    coupling,
    quad_index,
    quad_weight,
):
    comps_local, lat_rows, lon_cols = spectrum.shape
    n_comp = lax.axis_size("comp")
    n_lat = lax.axis_size("lat")
    deep_rim = 2 * SUBSTEPS
    stacked = jnp.stack([sea_mask, depth_class, current_class])
    padded = with_halo(stacked, (("lat", 1), ("lon", 2)), deep_rim)
    row_global = (
        lax.axis_index("lat") * lat_rows
        - deep_rim
        + jnp.arange(lat_rows + 2 * deep_rim, dtype=jnp.int32)
    )
    inside = ((row_global >= 0) & (row_global < lat_rows * n_lat)).astype(jnp.float32)[:, None]
    wet_rim = (padded[0].astype(jnp.float32) * inside)[None]
    comp_ids = lax.axis_index("comp") * comps_local + jnp.arange(comps_local, dtype=jnp.int32)
    cour_x, cour_y = courant(comp_ids, padded[1], padded[2], speed_table, current_table)
    energy = spectrum * sea_mask.astype(jnp.float32)[None]
    inner_rows = inside[deep_rim - 2 : deep_rim + lat_rows + 2]
    offset = deep_rim - 2
    for substep in range(SUBSTEPS):
        rimmed = with_halo(energy, (("lat", 1), ("lon", 2)), 2) * inner_rows[None]
        energy = advance(
            rimmed, window(cour_x, offset), window(cour_y, offset), window(wet_rim, offset)
        )
    kernel_plus = dense_kernel(quad_index[0], quad_weight[0])
    kernel_minus = dense_kernel(quad_index[1], quad_weight[1])
    cell_count = lat_rows * lon_cols
    outgoing = energy.reshape(comps_local, n_comp, cell_count // n_comp)
    pieces = lax.all_to_all(outgoing, "comp", split_axis=1, concat_axis=0, tiled=True)
    point_grid = pieces.reshape(pieces.shape[0], pieces.shape[2])
    arrived = interact(point_grid, kernel_plus, kernel_minus, coupling).reshape(pieces.shape)
    returned = lax.all_to_all(arrived, "comp", split_axis=0, concat_axis=1, tiled=True)
    return returned.reshape(comps_local, lat_rows, lon_cols)


CHUNK = 24
BLOCK = 12
TILE = 128
MESH = pl.DeviceIdType.MESH


def limited(upper, lower):
    return jnp.maximum(
        jnp.minimum(upper, lower), jnp.minimum(jnp.maximum(upper, lower), 0.0)
    )


def aligned(index, unit):
    return pl.multiple_of(index, unit)


def step_kernel(
    nz,
    nx,
    nc,
    spec,
    sea_mask,
    depth_class,
    current_class,
    coupling,
    quad_index,
    quad_weight,
    speed_table,
    current_table,
    turns,
    out,
    gbuf,
    buf,
    fields,
    base,
    send,
    arrived,
    low,
    kern,
    kern_t,
    strength,
    source,
    source_low,
    result,
    returned,
    sem_grid_s,
    sem_grid_r,
    sem_a_s,
    sem_a_r,
    sem_c_s,
    sem_c_r,
    sem_d_s,
    sem_d_r,
):
    z, x, c = lax.axis_index("comp"), lax.axis_index("lat"), lax.axis_index("lon")
    group = nx * nc
    me = x * nc + c
    rows, cols = returned.shape[0], returned.shape[2]
    comps_local = returned.shape[1]
    comps_own = buf.shape[1] // rows
    comp_total = arrived.shape[1]
    row_share = rows // nz
    chunks = comps_own // CHUNK
    all_rows, all_cols = rows * nx, cols * nc

    def place(dz, dg):
        other = lax.rem(me + dg, group)
        return lax.rem(z + dz, nz), other, {
            "comp": lax.rem(z + dz, nz),
            "lat": other // nc,
            "lon": lax.rem(other, nc),
        }

    barrier = pltpu.get_barrier_semaphore()
    for dz in range(nz):
        for dg in range(group):
            if dz or dg:
                _, _, there = place(dz, dg)
                pl.semaphore_signal(barrier, inc=1, device_id=there, device_id_type=MESH)
    pl.semaphore_wait(barrier, nz * group - 1)

    for i, grid in enumerate((sea_mask, depth_class, current_class)):
        pltpu.make_async_copy(grid, gbuf.at[me, i], sem_grid_r.at[me, i]).start()
        for dg in range(1, group):
            _, other, there = place(0, dg)
            pltpu.make_async_remote_copy(
                src_ref=grid,
                dst_ref=gbuf.at[me, i],
                send_sem=sem_grid_s.at[dg, i],
                recv_sem=sem_grid_r.at[me, i],
                device_id=there,
                device_id_type=MESH,
            ).start()
    span = CHUNK * rows

    @pl.loop(0, chunks)
    def _(ch):
        here = pl.ds(aligned(ch * span, span), span)
        for dg in range(group):
            _, other, there = place(0, dg)
            taken = pl.ds(aligned(other * (comps_own * rows) + ch * span, span), span)
            if dg == 0:
                pltpu.make_async_copy(
                    spec.at[taken], buf.at[me, here], sem_a_r.at[me, ch]
                ).start()
            else:
                pltpu.make_async_remote_copy(
                    src_ref=spec.at[taken],
                    dst_ref=buf.at[me, here],
                    send_sem=sem_a_s.at[dg, ch],
                    recv_sem=sem_a_r.at[me, ch],
                    device_id=there,
                    device_id_type=MESH,
                ).start()

    lanes = lax.broadcasted_iota(jnp.int32, (TILE, TILE), 1)
    subs = lax.broadcasted_iota(jnp.int32, (TILE, TILE), 0)

    def make_dense(t):
        start = aligned(t * TILE, TILE)
        spot = pl.ds(start, TILE)
        strength[spot, :] = jnp.broadcast_to(coupling[pl.ds(t, 1), :], (cols, TILE)).T
        indices, weights = (
            jnp.concatenate(
                [table[side, :, spot].astype(jnp.float32) for side in range(2)], axis=0
            ).T
            for table in (quad_index, quad_weight)
        )
        indices = indices.astype(jnp.int32)
        for side in range(2):
            for left in range(0, comp_total, TILE):
                block = jnp.zeros((TILE, TILE), jnp.float32)
                for corner in range(4):
                    one = slice(side * 4 + corner, side * 4 + corner + 1)
                    block = jnp.where(lanes + left == indices[:, one], weights[:, one], block)
                kern[side, spot, left : left + TILE] = block.astype(jnp.bfloat16)

    def make_dense_t(t):
        start = aligned(t * TILE, TILE)
        spot = pl.ds(start, TILE)
        for left in range(0, comp_total, TILE):
            part = slice(left, left + TILE)
            both = []
            for side in range(2):
                block = jnp.zeros((TILE, TILE), jnp.float32)
                for corner in range(4):
                    one = slice(corner, corner + 1)
                    block = jnp.where(
                        subs + start == quad_index[side, one, part],
                        quad_weight[side, one, part],
                        block,
                    )
                both.append(block)
            kern_t[spot, part] = (both[0] + both[1]).astype(jnp.bfloat16)

    for g in range(group):
        for i in range(3):
            pltpu.make_async_copy(gbuf.at[g, i], gbuf.at[g, i], sem_grid_r.at[g, i]).wait()

    def whole(pick):
        return jnp.concatenate(
            [
                jnp.concatenate([pick(i * nc + j) for j in range(nc)], axis=1)
                for i in range(nx)
            ],
            axis=0,
        )

    row_ids = lax.broadcasted_iota(jnp.int32, (all_rows, all_cols), 0)

    def east(v):
        return pltpu.roll(v, all_cols - 1, 1)

    def west(v):
        return pltpu.roll(v, 1, 1)

    def north(v):
        return jnp.where(row_ids < all_rows - 1, pltpu.roll(v, all_rows - 1, 0), 0.0)

    def south(v):
        return jnp.where(row_ids > 0, pltpu.roll(v, 1, 0), 0.0)

    wet = whole(lambda g: gbuf[g, 0]).astype(jnp.float32)
    depth = whole(lambda g: gbuf[g, 1])
    current = whole(lambda g: gbuf[g, 2])
    wet_x = 0.5 * (wet * east(wet))
    wet_y = 0.5 * (wet * north(wet))
    flow_x = jnp.zeros_like(wet)
    flow_y = jnp.zeros_like(wet)
    for n in range(current_table.shape[1]):
        flow_x = jnp.where(current == n, current_table[0, n], flow_x)
        flow_y = jnp.where(current == n, current_table[1, n], flow_y)
    base[0] = (flow_x + east(flow_x)) * wet_x
    base[1] = (flow_y + north(flow_y)) * wet_y
    base[2] = wet
    first_freq = (z * comps_local + me * comps_own) // NDIR
    for j in range(comps_own // NDIR):
        speed = jnp.zeros_like(wet)
        for n in range(speed_table.shape[0]):
            speed = jnp.where(depth == n, speed_table[n, first_freq + j], speed)
        fields[j, 0] = (speed + east(speed)) * wet_x
        fields[j, 1] = (speed + north(speed)) * wet_y

    def propagate(first):
        freq = first // NDIR
        angle = lax.rem(first, NDIR)
        for k in range(BLOCK):
            spot = pl.ds(aligned((first + k) * rows, rows), rows)
            energy = whole(lambda g: buf[g, spot, :]) * base[2]
            speed_x = fields[freq, 0] * turns[0, angle + k] + base[0]
            speed_y = fields[freq, 1] * turns[1, angle + k] + base[1]
            size_x, size_y = jnp.abs(speed_x), jnp.abs(speed_y)
            half_x = 0.5 * size_x * (1.0 - size_x)
            half_y = 0.5 * size_y * (1.0 - size_y)
            for _ in range(SUBSTEPS):
                ahead, behind = east(energy), west(energy)
                slope = limited(ahead - energy, energy - behind)
                flux_x = speed_x * jnp.where(speed_x > 0.0, energy, ahead) + half_x * jnp.where(
                    speed_x > 0.0, slope, east(slope)
                )
                ahead, behind = north(energy), south(energy)
                slope = limited(ahead - energy, energy - behind)
                flux_y = speed_y * jnp.where(speed_y > 0.0, energy, ahead) + half_y * jnp.where(
                    speed_y > 0.0, slope, pltpu.roll(slope, all_rows - 1, 0)
                )
                energy = (
                    energy - (flux_x - west(flux_x)) - (flux_y - pltpu.roll(flux_y, 1, 0))
                )
            for i in range(nx):
                for j in range(nc):
                    buf[i * nc + j, spot, :] = energy[
                        i * rows : (i + 1) * rows, j * cols : (j + 1) * cols
                    ]

    own_first = (z * group + me) * comps_own

    def pass_on(row, start, count, sem_row):
        there_spot = pl.ds(aligned(own_first + start, 8), count)
        here_spot = pl.ds(aligned(start, 8), count)
        for dz in (2, 1, 3, 0) if nz == 4 else range(nz):
            for dg in range(group):
                to_z, other, there = place(dz, dg)
                piece = send.at[other, to_z * row_share + row, here_spot]
                target = arrived.at[row, there_spot]
                if dz or dg:
                    pltpu.make_async_remote_copy(
                        src_ref=piece,
                        dst_ref=target,
                        send_sem=sem_c_s.at[row],
                        recv_sem=sem_c_r.at[row],
                        device_id=there,
                        device_id_type=MESH,
                    ).start()
                else:
                    pltpu.make_async_copy(piece, target, sem_c_r.at[row]).start()

    @pl.loop(0, chunks)
    def _(ch):
        here = pl.ds(aligned(ch * span, span), span)
        for g in range(group):
            pltpu.make_async_copy(
                buf.at[g, here], buf.at[g, here], sem_a_r.at[g, ch]
            ).wait()

        @pl.loop(0, CHUNK // BLOCK)
        def _(b):
            propagate(ch * CHUNK + b * BLOCK)

        for g in range(group):
            for row in range(rows):
                send[g, row, pl.ds(aligned(ch * CHUNK, 8), CHUNK), :] = buf[
                    g, pl.ds(ch * span + row, CHUNK, stride=rows), :
                ]
        pass_on(0, ch * CHUNK, CHUNK, 0)

    for row in range(1, row_share):
        pass_on(row, 0, comps_own, row)

    pl.loop(0, comp_total // TILE)(make_dense)
    pl.loop(0, comp_total // TILE)(make_dense_t)

    for row in range(row_share):
        pltpu.make_async_copy(arrived.at[row], arrived.at[row], sem_c_r.at[row]).wait()
        low[...] = arrived[row].astype(jnp.bfloat16)

        @pl.loop(0, comp_total // TILE)
        def _(t):
            spot = pl.ds(aligned(t * TILE, TILE), TILE)
            plus = jnp.dot(kern[0, spot, :], low[...], preferred_element_type=jnp.float32)
            minus = jnp.dot(kern[1, spot, :], low[...], preferred_element_type=jnp.float32)
            energy = arrived[row, spot, :]
            gain = strength[spot, :] * (
                energy * energy * (plus_factor * plus + minus_factor * minus)
                - cross_factor * energy * plus * minus
            )
            source[spot, :] = gain
            source_low[spot, :] = gain.astype(jnp.bfloat16)

        for dz in (2, 1, 3, 0) if nz == 4 else range(nz):
            to_z, _, there = place(dz, 0)
            first = to_z * comps_local

            @pl.loop(0, comps_local // 96)
            def _(t):
                spot = pl.ds(aligned(first + t * 96, 32), 96)
                net = (
                    jnp.dot(kern_t[spot, :], source_low[...], preferred_element_type=jnp.float32)
                    - 2.0 * source[spot, :]
                )
                result[row, spot, :] = arrived[row, spot, :] + net / (1.0 + jnp.abs(net))

            piece = result.at[row, pl.ds(aligned(first, 8), comps_local)]
            target = returned.at[z * row_share + row]
            if dz:
                pltpu.make_async_remote_copy(
                    src_ref=piece,
                    dst_ref=target,
                    send_sem=sem_d_s.at[row],
                    recv_sem=sem_d_r.at[row],
                    device_id=there,
                    device_id_type=MESH,
                ).start()
            else:
                pltpu.make_async_copy(piece, target, sem_d_r.at[row]).start()

    for row in range(row_share):
        all_z = returned.at[pl.ds(0, nz)]
        pltpu.make_async_copy(all_z, all_z, sem_d_r.at[row]).wait()
        for quarter in range(nz):
            line = quarter * row_share + row
            out[pl.ds(line, comps_local, stride=rows), :] = returned[line]

    for dg in range(1, group):
        for i in range(3):
            pltpu.make_async_copy(gbuf.at[0, i], gbuf.at[0, i], sem_grid_s.at[dg, i]).wait()

        @pl.loop(0, chunks)
        def _(ch):
            here = pl.ds(0, span)
            pltpu.make_async_copy(buf.at[0, here], buf.at[0, here], sem_a_s.at[dg, ch]).wait()

    for row in range(row_share):
        sent = arrived.at[row, pl.ds(0, comp_total - comps_own)]
        pltpu.make_async_copy(sent, sent, sem_c_s.at[row]).wait()
        sent = returned.at[pl.ds(0, nz - 1)]
        pltpu.make_async_copy(sent, sent, sem_d_s.at[row]).wait()


def fused(nz, nx, nc, *arrays):
    (
        spectrum,
        sea_mask,
        depth_class,
        current_class,
        speed_table,
        current_table,
        coupling,
        quad_index,
        quad_weight,
    ) = arrays
    comps_local, rows, cols = spectrum.shape
    comp_total = coupling.shape[0]
    group = nx * nc
    own = comps_local // group
    share = rows // nz
    turn = 2.0 * math.pi / NDIR * np.arange(NDIR)
    turns = jnp.asarray(np.stack([np.cos(turn), np.sin(turn)]), jnp.float32)
    vmem = pl.BlockSpec(memory_space=pltpu.VMEM)
    smem = pl.BlockSpec(memory_space=pltpu.SMEM)
    f32, bf16, i32 = jnp.float32, jnp.bfloat16, jnp.int32
    dma = pltpu.SemaphoreType.DMA
    out = pl.pallas_call(
        functools.partial(step_kernel, nz, nx, nc),
        name="wave_step",
        out_shape=jax.ShapeDtypeStruct((comps_local * rows, cols), f32),
        in_specs=[pl.BlockSpec(memory_space=pl.ANY)] + [vmem] * 6 + [smem] * 3,
        out_specs=vmem,
        scratch_shapes=[
            pltpu.VMEM((group, 3, rows, cols), i32),
            pltpu.VMEM((group, own * rows, cols), f32),
            pltpu.VMEM((own // NDIR, 2, rows * nx, cols * nc), f32),
            pltpu.VMEM((3, rows * nx, cols * nc), f32),
            pltpu.VMEM((group, rows, own, cols), f32),
            pltpu.VMEM((share, comp_total, cols), f32),
            pltpu.VMEM((comp_total, cols), bf16),
            pltpu.VMEM((2, comp_total, comp_total), bf16),
            pltpu.VMEM((comp_total, comp_total), bf16),
            pltpu.VMEM((comp_total, cols), f32),
            pltpu.VMEM((comp_total, cols), f32),
            pltpu.VMEM((comp_total, cols), bf16),
            pltpu.VMEM((share, comp_total, cols), f32),
            pltpu.VMEM((rows, comps_local, cols), f32),
            dma((group, 3)),
            dma((group, 3)),
            dma((group, own // CHUNK)),
            dma((group, own // CHUNK)),
            dma((share,)),
            dma((share,)),
            dma((share,)),
            dma((share,)),
        ],
        compiler_params=pltpu.CompilerParams(
            collective_id=0, has_side_effects=True, vmem_limit_bytes=60 * 1024 * 1024
        ),
    )(
        spectrum.reshape(comps_local * rows, cols),
        sea_mask,
        depth_class,
        current_class,
        coupling.reshape(comp_total // TILE, TILE),
        quad_index.transpose(0, 2, 1),
        quad_weight.transpose(0, 2, 1),
        speed_table,
        current_table.T,
        turns,
    )
    return out.reshape(comps_local, rows, cols)


def step(*arrays):
    comps_local, rows, cols = arrays[0].shape
    comp_total = arrays[6].shape[0]
    nz, nx, nc = (lax.axis_size(a) for a in ("comp", "lat", "lon"))
    own = comps_local // (nx * nc)
    fits = (
        comps_local % (nx * nc) == 0
        and own % NDIR == 0
        and own % CHUNK == 0
        and CHUNK % BLOCK == 0
        and NDIR % BLOCK == 0
        and rows == 8
        and cols == TILE
        and rows % nz == 0
        and comp_total % TILE == 0
        and comps_local % 96 == 0
    )
    return fused(nz, nx, nc, *arrays) if fits else local(*arrays)


def solution(mesh):
    placed = (
        P(("ens", "comp"), "lat", "lon"),
        P("lat", "lon"),
        P("lat", "lon"),
        P("lat", "lon"),
        P(),
        P(),
        P(),
        P(),
        P(),
    )
    return jax.shard_map(
        step,
        mesh=mesh,
        in_specs=placed,
        out_specs=P(("ens", "comp"), "lat", "lon"),
        check_vma=False,
    )
```
